32 devices in a mesh: tm: 8 (over z, core), dp: 2 (over y), rep: 2 (over x).
Axes of the slice: x: 2, y: 2, z: 4, core: 2. Of those that a mesh axis runs over, the one named last changes fastest.
Arguments:
- clip_frames: bfloat16 [4, 32, 8, 4, 256], P(('dp', 'rep'), 'tm'), may hold values from -6 to 6
- conv_weight: bfloat16 [3, 3, 3, 256, 256], replicated, may hold values from -0.078125 to 0.078125
- up_weight: bfloat16 [256, 1024], replicated, may hold values from -0.375 to 0.375
- cotangent: bfloat16 [4, 32, 8, 4, 1024], P(('dp', 'rep'), None, 'tm'), may hold values from -6 to 6
Outputs:
- input_grad: bfloat16 [4, 32, 8, 4, 256], P(('dp', 'rep'), 'tm')
- up_grad: float32 [256, 1024], P('tm', ('dp', 'rep'))
The draws below stay inside these ranges and needn't reach their ends.
All inputs are finite; a program needn't handle non-finite values.
Results may differ from the reference program's by a relative error of at most 0.012.
Values may be sent and summed in bfloat16 or wider, within the bound.
No kernel may reach another device: no remote copies, remote signals or barrier semaphores. Data moves between devices by JAX's collectives and lax.ppermute only.
A program may use at most 128 MiB of HBM per device.

```python
import math
import jax
import jax.numpy as jnp
from jax import lax

C = 256
COLS = 4
CUP = 1024
T_SIZE = 32
H = 8
CLIPS = 4


def spiked(values, own_key, source, target, parts, factor):
    owner, partner = [(jnp.arange(values.shape[dim]) // (values.shape[dim] // parts)).reshape([-1 if axis == dim else 1 for axis in range(values.ndim)]) for dim in (source, target)]
    chosen = jax.random.permutation(own_key, parts)[partner]
    strong = (owner == chosen) | (owner == (partner + parts // 2) % parts)
    return jnp.where(strong, factor * values, values)


def shard_levels(rng, dims, cuts, low, largest):
    def one(dim, shards_of):
        steps = jax.random.uniform(jax.random.fold_in(jax.random.fold_in(rng, 6), dim), (shards_of,), jnp.float32, low / len(cuts), largest / len(cuts))
        return jnp.repeat(jnp.exp(steps), dims[dim] // shards_of).reshape((-1,) + (1,) * (len(dims) - dim - 1))

    loudness = one(*cuts[0])
    for cut in cuts[1:]:
        loudness = loudness * one(*cut)
    return loudness


def noise(own_key, dims, deviation, most, split=(), dtype=jnp.bfloat16):
    gain = shard_levels(own_key, dims, split, -0.22, 0.18) if split else 1.0
    drawn = jax.random.normal(own_key, dims, jnp.float32) * deviation * gain
    return jnp.minimum(jnp.maximum(drawn, -most), most).astype(dtype)


def gaussian_with(key, extent, scale, most, shards, heavy, dtype=jnp.bfloat16):
    array = scale * jax.random.normal(key, extent, jnp.float32)
    if shards:
        array = array * shard_levels(key, extent, shards, -0.22, 0.18)
    return jnp.clip(spiked(array, jax.random.fold_in(key, 3), *heavy), -most, most).astype(dtype)


def setup_inputs(seed: int = 0) -> dict:
    key_list = jax.random.split(jax.random.key(seed), 5)
    return {
        "clip_frames": noise(key_list[0], (CLIPS, T_SIZE, H, COLS, C), 1.0, 6.0, ((0, 4), (1, 8))),
        "conv_weight": noise(key_list[1], (3, 3, 3, C, C), (27 * C) ** -0.5, 0.078125),
        "up_weight": noise(key_list[2], (C, CUP), C ** -0.5, 0.375),
        "cotangent": gaussian_with(key_list[3], (CLIPS, T_SIZE, H, COLS, CUP), 1.0, 6.0, ((0, 4), (2, 8)), (0, 4, 4, 2.0)),
    }


def forward_pre(frames, kernel):
    padded = jnp.concatenate([frames[:1], frames[:1], frames], axis=0)
    result = lax.conv_general_dilated(padded[None], kernel, (1, 1, 1), [(0, 0), (1, 1), (1, 1)], dimension_numbers=('NDHWC', 'DHWIO', 'NDHWC'), precision=lax.Precision.HIGHEST)
    return result[0]

def reference(clip_frames, conv_weight, up_weight, cotangent):
    kernel = conv_weight.astype(jnp.float32)

    def one_clip(total, pair):
        frames, upstream = pair
        pre, pull = jax.vjp(lambda value: forward_pre(value, kernel), frames.astype(jnp.float32))
        flat_pre = pre.reshape(-1, C)
        hidden = jax.nn.silu(flat_pre).astype(jnp.bfloat16)
        flat_g = upstream.reshape(-1, upstream.shape[-1])
        term = lax.dot_general(hidden, flat_g, (((0,), (0,)), ((), ())), preferred_element_type=jnp.float32)
        hidden_grad = lax.dot_general(flat_g, up_weight, (((1,), (1,)), ((), ())), preferred_element_type=jnp.float32).astype(jnp.bfloat16)
        sigma = jax.nn.sigmoid(flat_pre)
        slope = sigma * (1.0 + flat_pre * (1.0 - sigma))
        pre_grad = (hidden_grad.astype(jnp.float32) * slope).astype(jnp.bfloat16)
        frame_grad, = pull(pre_grad.astype(jnp.float32).reshape(pre.shape))
        return (total + term, frame_grad.astype(jnp.bfloat16))
    total, input_grad = lax.scan(one_clip, jnp.zeros((C, 4 * C), jnp.float32), (clip_frames, cotangent))
    factor = 1.0 / math.sqrt(CLIPS * T_SIZE * H * COLS)
    return (input_grad, total * factor)
```

```python
import functools
import math

import jax
import jax.numpy as jnp
from jax import lax
from jax.experimental import pallas as pl
from jax.experimental.pallas import tpu as pltpu
from jax.sharding import PartitionSpec as P


F32 = jnp.float32
BF16 = jnp.bfloat16
IN_VMEM = pl.BlockSpec(memory_space=pltpu.VMEM)
IN_SMEM = pl.BlockSpec(memory_space=pltpu.SMEM)
IN_ANY = pl.BlockSpec(memory_space=pl.ANY)
NT = (((1,), (1,)), ((), ()))
TN = (((0,), (0,)), ((), ()))
DIRECT = 4


def struct(shape, dtype):
    return jax.ShapeDtypeStruct(shape, dtype)


def from_behind(value, axis, steps):
    count = lax.axis_size(axis)
    initial, last = (max(0, -steps), min(count, count - steps))
    return lax.ppermute(value, axis, [(source, source + steps) for source in range(initial, last)])


def swap(value, axis, mask):
    count = lax.axis_size(axis)
    return lax.ppermute(value, axis, [(source, source ^ mask) for source in range(count)])


def weight_copies(w_hbm, w_vmem, sems):
    return [
        pltpu.make_async_copy(w_hbm.at[pl.ds(3 * g, 3)], w_vmem.at[pl.ds(3 * g, 3)], sems.at[g])
        for g in range(9)
    ]


def patch(field, frames, pad, area, cols, shift_r, shift_c):
    start = pad + shift_r * cols + shift_c
    block = field[:frames, start : start + area, :]
    if shift_c:
        col = lax.broadcasted_iota(jnp.int32, block.shape, 1) % cols
        inside = (col + shift_c >= 0) & (col + shift_c < cols)
        block = jnp.where(inside, block, 0.0)
    return block.astype(BF16)


def padding(cols):
    return -(-(cols + 1) // 8) * 8


def clear_edges(field, pad):
    frames, length, chans = field.shape
    edge = jnp.zeros((frames, pad, chans), F32)
    field[:, 0:pad, :] = edge
    field[:, length - pad :, :] = edge


def forward_kernel(meta, earlier, frames_ref, w_hbm, hidden, slope, w_vmem, field, sems):
    frames, rows, cols, chans = frames_ref.shape
    area = rows * cols
    pad = padding(cols)
    copies = weight_copies(w_hbm, w_vmem, sems)
    for copy in copies:
        copy.start()
    clear_edges(field, pad)
    first = meta[0] == 0
    for t in range(frames + 2):
        for r in range(rows):
            if t < 2:
                value = jnp.where(first, frames_ref[0, r], earlier[t, r])
            else:
                value = frames_ref[t - 2, r]
            field[t, pad + r * cols : pad + (r + 1) * cols, :] = value.astype(F32)
    total = jnp.zeros((frames * area, chans), F32)
    patches = [
        [patch(field, frames + 2, pad, area, cols, b - 1, c - 1) for c in range(3)] for b in range(3)
    ]
    for a in range(3):
        for b in range(3):
            copies[3 * a + b].wait()
            for c in range(3):
                left = patches[b][c][a : a + frames].reshape(frames * area, chans)
                total += jnp.dot(left, w_vmem[9 * a + 3 * b + c], preferred_element_type=F32)
    sigma = 1.0 / (1.0 + jnp.exp(-total))
    hidden[...] = (total * sigma).astype(BF16)
    slope[...] = sigma * (1.0 + total * (1.0 - sigma))


def forward(meta, earlier, frames, weight):
    count, rows, cols, chans = frames.shape
    area = rows * cols
    return pl.pallas_call(
        forward_kernel,
        out_shape=(struct((count * area, chans), BF16), struct((count * area, chans), F32)),
        in_specs=[IN_SMEM, IN_VMEM, IN_VMEM, IN_ANY],
        out_specs=(IN_VMEM, IN_VMEM),
        scratch_shapes=[
            pltpu.VMEM(weight.shape, BF16),
            pltpu.VMEM((count + 2, area + 2 * padding(cols), chans), F32),
            pltpu.SemaphoreType.DMA((9,)),
        ],
        name="forward_conv",
    )(meta, earlier, frames, weight)


def middle_kernel(size, meta, g, up, hidden, slope, pre_grad, keep, send, term):
    hidden_grad = lax.dot_general(g[...], up[...], NT, preferred_element_type=F32).astype(BF16)
    pre_grad[...] = (hidden_grad.astype(F32) * slope[...]).astype(BF16)
    term[...] = lax.dot_general(hidden[...], g[...], TN, preferred_element_type=F32)
    parts, half, width = keep.shape
    mine = meta[0] % 2
    for m in range(half // size):
        kept = pl.ds(pl.multiple_of((2 * m + mine) * size, size), size)
        sent = pl.ds(pl.multiple_of((2 * m + 1 - mine) * size, size), size)
        for n in range(parts):
            lanes = slice(n * width, (n + 1) * width)
            keep[n, m * size : (m + 1) * size, :] = term[kept, lanes]
            send[n, m * size : (m + 1) * size, :] = term[sent, lanes].astype(BF16)


def middle(meta, g, up, hidden, slope, size, parts):
    chans, width = up.shape
    return pl.pallas_call(
        functools.partial(middle_kernel, size),
        out_shape=(
            struct(hidden.shape, BF16),
            struct((parts, chans // 2, width // parts), F32),
            struct((parts, chans // 2, width // parts), BF16),
        ),
        in_specs=[IN_SMEM] + [IN_VMEM] * 4,
        out_specs=(IN_VMEM,) * 3,
        scratch_shapes=[pltpu.VMEM((chans, width), F32)],
        name="middle",
    )(meta, g, up, hidden, slope)


def backward_kernel(meta, pre_grad, later, w_hbm, out, w_vmem, field, sems):
    frames, rows, cols, chans = out.shape
    area = rows * cols
    pad = padding(cols)
    copies = weight_copies(w_hbm, w_vmem, sems)
    for copy in copies:
        copy.start()
    clear_edges(field, pad)
    for t in range(frames + 2):
        source = pre_grad if t < frames else later
        base = (t if t < frames else t - frames) * area
        field[t, pad : pad + area, :] = source[base : base + area, :].astype(F32)
    patches = [
        [patch(field, frames + 2, pad, area, cols, 1 - b, 1 - c) for c in range(3)] for b in range(3)
    ]
    sums = []
    for a in range(3):
        count = (frames + 2 - a) * area
        total = jnp.zeros((count, chans), F32)
        for b in range(3):
            copies[3 * a + b].wait()
            for c in range(3):
                left = patches[b][c][: frames + 2 - a].reshape(count, chans)
                total += lax.dot_general(
                    left, w_vmem[9 * a + 3 * b + c], NT, preferred_element_type=F32
                )
        sums.append(total)
    edge = sums[0][:area] + sums[0][area : 2 * area] + sums[1][:area]
    edge = jnp.where(meta[0] == 0, edge, 0.0)
    value = sums[0][2 * area :] + sums[1][area:] + sums[2]
    for t in range(frames):
        frame = value[t * area : (t + 1) * area]
        if t == 0:
            frame = frame + edge
        for r in range(rows):
            out[t, r] = frame[r * cols : (r + 1) * cols].astype(BF16)


def backward(meta, pre_grad, later, weight, shape):
    count, rows, cols, chans = shape
    return pl.pallas_call(
        backward_kernel,
        out_shape=struct(shape, BF16),
        in_specs=[IN_SMEM, IN_VMEM, IN_VMEM, IN_ANY],
        out_specs=IN_VMEM,
        scratch_shapes=[
            pltpu.VMEM(weight.shape, BF16),
            pltpu.VMEM((count + 2, rows * cols + 2 * padding(cols), chans), F32),
            pltpu.SemaphoreType.DMA((9,)),
        ],
        name="backward_conv",
    )(meta, pre_grad, later, weight)


def split_kernel(keep, got, spot, mine, sends):
    me = spot[1]
    mine[...] = keep[me] + got[me].astype(F32)
    for k in range(1, keep.shape[0]):
        other = me ^ k
        sends[k - 1] = (keep[other] + got[other].astype(F32)).astype(BF16)


def split(meta, keep, got):
    parts, half, width = keep.shape

    def body(spot, keep, got, mine, sends):
        split_kernel(keep, got, spot, mine, sends)

    return pl.pallas_call(
        body,
        out_shape=(struct((half, width), F32), struct((parts - 1, half, width), BF16)),
        in_specs=[IN_SMEM, IN_VMEM, IN_VMEM],
        out_specs=(IN_VMEM, IN_VMEM),
        name="split_cols",
    )(meta, keep, got)


def spread_kernel(size, count, spot, mine, *refs):
    got, (kept, sends) = refs[:-2], refs[-2:]

    def total(block):
        rows = pl.ds(pl.multiple_of(block * size, size), size)
        value = mine[rows, :]
        for ref in got:
            value = value + ref[rows, :].astype(F32)
        return value

    me = spot[0] // 2
    kept[...] = total(me)
    for k in range(1, count):
        sends[k - 1] = total(me ^ k).astype(BF16)


def spread(meta, mine, got, size):
    half, width = mine.shape
    count = half // size
    return pl.pallas_call(
        functools.partial(spread_kernel, size, count),
        out_shape=(struct((size, width), F32), struct((count - 1, size, width), BF16)),
        in_specs=[IN_SMEM, IN_VMEM] + [IN_VMEM] * len(got),
        out_specs=(IN_VMEM, IN_VMEM),
        name="split_rows",
    )(meta, mine, *got)


def final_kernel(factor, mine, *refs):
    value = mine[...]
    for ref in refs[:-1]:
        value = value + ref[...].astype(F32)
    refs[-1][...] = value * factor


def final(mine, got, factor):
    return pl.pallas_call(
        functools.partial(final_kernel, factor),
        out_shape=struct(mine.shape, F32),
        in_specs=[IN_VMEM] * (1 + len(got)),
        out_specs=IN_VMEM,
        name="final_sum",
    )(mine, *got)


def local(clip_frames, conv_weight, up_weight, cotangent):
    frames_local = clip_frames[0]
    frames, rows, cols, chans = frames_local.shape
    width = up_weight.shape[1]
    time_count = lax.axis_size("tm")
    clip_count = lax.axis_size(("dp", "rep"))
    area = rows * cols
    spot = lax.axis_index("tm")
    meta = jnp.stack([spot, lax.axis_index(("dp", "rep"))]).astype(jnp.int32)
    weight = conv_weight.reshape(27, chans, chans)
    factor = 1.0 / math.sqrt(clip_count * frames * time_count * area)
    size = chans // time_count

    earlier = from_behind(frames_local[frames - 2 :], "tm", 1)
    frame_cot = lax.all_to_all(cotangent, "tm", split_axis=1, concat_axis=2, tiled=True)
    hidden, slope = forward(meta, earlier, frames_local, weight)
    flat_g = frame_cot.reshape(frames * area, width)
    pre_grad, keep, send = middle(meta, flat_g, up_weight, hidden, slope, size, clip_count)
    later = from_behind(pre_grad[: 2 * area], "tm", -1)
    got = swap(send, "tm", 1)
    if clip_count <= DIRECT and time_count // 2 <= DIRECT:
        mine, sends = split(meta, keep, got)
        arrived = [swap(sends[k - 1], ("dp", "rep"), k) for k in range(1, clip_count)]
        kept, sends = spread(meta, mine, arrived, size)
        arrived = [swap(sends[k - 1], "tm", 2 * k) for k in range(1, time_count // 2)]
        summed = final(kept, arrived, factor)
    else:
        value = keep + got.astype(F32)
        value = lax.psum_scatter(value, ("dp", "rep"), scatter_dimension=0, tiled=True)[0]
        pairs = [[s for s in range(time_count) if s % 2 == c] for c in range(2)]
        value = lax.psum_scatter(
            value, "tm", scatter_dimension=0, axis_index_groups=pairs, tiled=True
        )
        summed = value * factor
    input_grad = backward(meta, pre_grad, later, weight, frames_local.shape)
    return (input_grad[None], summed)


def solution(mesh):
    in_specs = (
        P(("dp", "rep"), "tm", None, None, None),
        P(),
        P(),
        P(("dp", "rep"), None, "tm", None, None),
    )
    out_specs = (P(("dp", "rep"), "tm", None, None, None), P("tm", ("dp", "rep")))
    return jax.shard_map(local, mesh=mesh, in_specs=in_specs, out_specs=out_specs, check_vma=False)
```

```python
import functools
import math

import jax
import jax.numpy as jnp
from jax import lax
from jax.experimental import pallas as pl
from jax.experimental.pallas import tpu as pltpu
from jax.sharding import PartitionSpec as P


F32 = jnp.float32
BF16 = jnp.bfloat16
IN_VMEM = pl.BlockSpec(memory_space=pltpu.VMEM)
IN_SMEM = pl.BlockSpec(memory_space=pltpu.SMEM)
NT = (((1,), (1,)), ((), ()))
TN = (((0,), (0,)), ((), ()))
DIRECT = 4
MIB = 1024 * 1024


def limit(mib):
    return pltpu.CompilerParams(vmem_limit_bytes=mib * MIB)


def struct(shape, dtype):
    return jax.ShapeDtypeStruct(shape, dtype)


def from_behind(value, axis, steps):
    count = lax.axis_size(axis)
    initial, last = (max(0, -steps), min(count, count - steps))
    return lax.ppermute(value, axis, [(source, source + steps) for source in range(initial, last)])


def swap(value, axis, mask):
    count = lax.axis_size(axis)
    return lax.ppermute(value, axis, [(source, source ^ mask) for source in range(count)])


def here():
    return lax.axis_index("tm")


def column_shift(block, cols, shift):
    if shift:
        col = lax.broadcasted_iota(jnp.int32, block.shape, 1) % cols
        inside = (col + shift >= 0) & (col + shift < cols)
        block = jnp.where(inside, block, 0.0)
    return block.astype(BF16)


def row_shift(flat, span, shift):
    edge = jnp.zeros((span, flat.shape[1]), flat.dtype)
    if shift < 0:
        return jnp.concatenate([edge, flat[:-span]], axis=0)
    if shift > 0:
        return jnp.concatenate([flat[span:], edge], axis=0)
    return flat


def forward_kernel(earlier, frames_ref, weight, hidden, slope, field):
    frames, rows, cols, chans = frames_ref.shape
    span = frames * cols
    first = here() == 0
    for r in range(rows):
        for t in range(frames + 2):
            if t < 2:
                value = jnp.where(first, frames_ref[0, r], earlier[frames - 2 + t, r])
            else:
                value = frames_ref[t - 2, r]
            field[r, 8 + t * cols : 8 + (t + 1) * cols, :] = value.astype(F32)
    total = jnp.zeros((rows * span, chans), F32)
    for a in range(3):
        flats = []
        for c in range(3):
            start = 8 + a * cols + c - 1
            block = column_shift(field[:, start : start + span, :], cols, c - 1)
            flats.append(block.reshape(rows * span, chans))
        left = jnp.concatenate(
            [row_shift(flats[c], span, b - 1) for b in range(3) for c in range(3)], axis=1
        )
        right = weight[9 * a : 9 * a + 9].reshape(9 * chans, chans)
        total += jnp.dot(left, right, preferred_element_type=F32)
    sigma = 1.0 / (1.0 + jnp.exp(-total))
    hidden[...] = (total * sigma).astype(BF16)
    slope[...] = sigma * (1.0 + total * (1.0 - sigma))


def forward(earlier, frames, weight):
    count, rows, cols, chans = frames.shape
    places = count * rows * cols
    length = -(-((count + 2) * cols + 9) // 8) * 8
    return pl.pallas_call(
        forward_kernel,
        out_shape=(struct((places, chans), BF16), struct((places, chans), F32)),
        in_specs=[IN_VMEM] * 3,
        out_specs=(IN_VMEM, IN_VMEM),
        scratch_shapes=[pltpu.VMEM((rows, length, chans), F32)],
        name="forward_conv",
        compiler_params=limit(12),
    )(earlier, frames, weight)


def middle_kernel(size, g_ref, up, hidden, slope, pre_grad, head, keep, send, flat, term):
    rows, frames, cols, width = g_ref.shape
    for r in range(rows):
        for t in range(frames):
            base = (r * frames + t) * cols
            flat[base : base + cols, :] = g_ref[r, t].astype(F32)
    g = flat[...].astype(BF16)
    hidden_grad = lax.dot_general(g, up[...], NT, preferred_element_type=F32).astype(BF16)
    value = (hidden_grad.astype(F32) * slope[...]).astype(BF16).reshape(pre_grad.shape)
    pre_grad[...] = value
    head[...] = value[:, : head.shape[1], :]
    term[...] = lax.dot_general(hidden[...], g, TN, preferred_element_type=F32)
    parts, half, lanes = keep.shape
    mine = here() % 2
    for m in range(half // size):
        kept = pl.ds(pl.multiple_of((2 * m + mine) * size, size), size)
        sent = pl.ds(pl.multiple_of((2 * m + 1 - mine) * size, size), size)
        for n in range(parts):
            cut = slice(n * lanes, (n + 1) * lanes)
            keep[n, m * size : (m + 1) * size, :] = term[kept, cut]
            send[n, m * size : (m + 1) * size, :] = term[sent, cut].astype(BF16)


def middle(g, up, hidden, slope, size, parts):
    chans, width = up.shape
    rows, frames, cols, _ = g.shape
    return pl.pallas_call(
        functools.partial(middle_kernel, size),
        out_shape=(
            struct((rows, frames * cols, chans), BF16),
            struct((rows, 2 * cols, chans), BF16),
            struct((parts, chans // 2, width // parts), F32),
            struct((parts, chans // 2, width // parts), BF16),
        ),
        in_specs=[IN_VMEM] * 4,
        out_specs=(IN_VMEM,) * 4,
        scratch_shapes=[
            pltpu.VMEM((rows * frames * cols, width), F32),
            pltpu.VMEM((chans, width), F32),
        ],
        name="middle",
        compiler_params=limit(12),
    )(g, up, hidden, slope)


def backward_kernel(pre_grad, later, weight, out, field):
    frames, rows, cols, chans = out.shape
    span = frames * cols
    field[:, 8 : 8 + span, :] = pre_grad[...].astype(F32)
    field[:, 8 + span : 8 + span + 2 * cols, :] = later[...].astype(F32)
    sums = []
    for a in range(3):
        size = (frames + 2 - a) * cols
        size = -(-size // 16) * 16
        total = jnp.zeros((rows * size, chans), F32)
        flats = []
        for c in range(3):
            start = 8 + 1 - c
            block = column_shift(field[:, start : start + size, :], cols, 1 - c)
            flats.append(block.reshape(rows * size, chans))
        for b in range(3):
            for c in range(3):
                left = row_shift(flats[c], size, 1 - b)
                total += lax.dot_general(
                    left, weight[9 * a + 3 * b + c], NT, preferred_element_type=F32
                )
        sums.append(total.reshape(rows, size, chans))
    edge = sums[0][:, :cols] + sums[0][:, cols : 2 * cols] + sums[1][:, :cols]
    edge = jnp.where(here() == 0, edge, 0.0)
    for t in range(frames):
        at = [slice((t + 2 - a) * cols, (t + 3 - a) * cols) for a in range(3)]
        frame = sums[0][:, at[0]] + sums[1][:, at[1]] + sums[2][:, at[2]]
        if t == 0:
            frame = frame + edge
        out[t] = frame.astype(BF16)


def backward(pre_grad, later, weight, shape):
    count, rows, cols, chans = shape
    length = 8 + -(-(count + 2) * cols // 16) * 16 + 8
    return pl.pallas_call(
        backward_kernel,
        out_shape=struct(shape, BF16),
        in_specs=[IN_VMEM] * 3,
        out_specs=IN_VMEM,
        scratch_shapes=[pltpu.VMEM((rows, length, chans), F32)],
        name="backward_conv",
        compiler_params=limit(12),
    )(pre_grad, later, weight)


def split_kernel(keep, got, mine, *sends):
    me = lax.axis_index(("dp", "rep"))
    mine[...] = keep[me] + got[me].astype(F32)
    for k, send in enumerate(sends, 1):
        send[...] = (keep[me ^ k] + got[me ^ k].astype(F32)).astype(BF16)


def split(keep, got):
    parts, half, width = keep.shape
    return pl.pallas_call(
        split_kernel,
        out_shape=(struct((half, width), F32),) + (struct((half, width), BF16),) * (parts - 1),
        in_specs=[IN_VMEM] * 2,
        out_specs=(IN_VMEM,) * parts,
        name="split_cols",
        compiler_params=limit(4),
    )(keep, got)


def spread_kernel(size, received, mine, *refs):
    got, kept, sends = refs[:received], refs[received], refs[received + 1 :]

    def total(block):
        rows = pl.ds(pl.multiple_of(block * size, size), size)
        value = mine[rows, :]
        for ref in got:
            value = value + ref[rows, :].astype(F32)
        return value

    me = here() // 2
    kept[...] = total(me)
    for k, send in enumerate(sends, 1):
        send[...] = total(me ^ k).astype(BF16)


def spread(mine, got, size):
    half, width = mine.shape
    count = half // size
    return pl.pallas_call(
        functools.partial(spread_kernel, size, len(got)),
        out_shape=(struct((size, width), F32),) + (struct((size, width), BF16),) * (count - 1),
        in_specs=[IN_VMEM] * (1 + len(got)),
        out_specs=(IN_VMEM,) * count,
        name="split_rows",
        compiler_params=limit(4),
    )(mine, *got)


def final_kernel(factor, mine, *refs):
    value = mine[...]
    for ref in refs[:-1]:
        value = value + ref[...].astype(F32)
    refs[-1][...] = value * factor


def final(mine, got, factor):
    return pl.pallas_call(
        functools.partial(final_kernel, factor),
        out_shape=struct(mine.shape, F32),
        in_specs=[IN_VMEM] * (1 + len(got)),
        out_specs=IN_VMEM,
        name="final_sum",
        compiler_params=limit(4),
    )(mine, *got)


def local(clip_frames, conv_weight, up_weight, cotangent):
    frames_local = clip_frames[0]
    frames, rows, cols, chans = frames_local.shape
    width = up_weight.shape[1]
    time_count = lax.axis_size("tm")
    clip_count = lax.axis_size(("dp", "rep"))
    weight = conv_weight.reshape(27, chans, chans)
    factor = 1.0 / math.sqrt(clip_count * frames * time_count * rows * cols)
    size = chans // time_count

    earlier = from_behind(frames_local, "tm", 1)
    own_rows = rows // time_count
    g = cotangent.reshape(time_count, frames, own_rows, cols, width).transpose(0, 2, 1, 3, 4)
    g = lax.all_to_all(g, "tm", split_axis=0, concat_axis=0, tiled=True)
    g = g.reshape(rows, frames, cols, width)
    hidden, slope = forward(earlier, frames_local, weight)
    pre_grad, head, keep, send = middle(g, up_weight, hidden, slope, size, clip_count)
    got = swap(send, "tm", 1)
    later = from_behind(head, "tm", -1)
    if clip_count <= DIRECT and time_count // 2 <= DIRECT:
        mine, *sends = split(keep, got)
        arrived = [swap(sends[k - 1], ("dp", "rep"), k) for k in range(1, clip_count)]
        kept, *sends = spread(mine, arrived, size)
        arrived = [swap(sends[k - 1], "tm", 2 * k) for k in range(1, time_count // 2)]
        summed = final(kept, arrived, factor)
    else:
        value = keep + got.astype(F32)
        value = lax.psum_scatter(value, ("dp", "rep"), scatter_dimension=0, tiled=True)[0]
        pairs = [[s for s in range(time_count) if s % 2 == c] for c in range(2)]
        value = lax.psum_scatter(
            value, "tm", scatter_dimension=0, axis_index_groups=pairs, tiled=True
        )
        summed = value * factor
    input_grad = backward(pre_grad, later, weight, frames_local.shape)
    return (input_grad[None], summed)


def solution(mesh):
    in_specs = (
        P(("dp", "rep"), "tm", None, None, None),
        P(),
        P(),
        P(("dp", "rep"), None, "tm", None, None),
    )
    out_specs = (P(("dp", "rep"), "tm", None, None, None), P("tm", ("dp", "rep")))
    return jax.shard_map(local, mesh=mesh, in_specs=in_specs, out_specs=out_specs, check_vma=False)
```

```python
import functools
import math

import jax
import jax.numpy as jnp
from jax import lax
from jax.experimental import pallas as pl
from jax.experimental.pallas import tpu as pltpu
from jax.sharding import PartitionSpec as P


F32 = jnp.float32
BF16 = jnp.bfloat16
IN_VMEM = pl.BlockSpec(memory_space=pltpu.VMEM)
IN_HBM = pl.BlockSpec(memory_space=pltpu.HBM)
NT = (((1,), (1,)), ((), ()))
TN = (((0,), (0,)), ((), ()))
DIRECT = 4
MIB = 1024 * 1024


def limit(mib):
    return pltpu.CompilerParams(vmem_limit_bytes=mib * MIB)


def struct(shape, dtype):
    return jax.ShapeDtypeStruct(shape, dtype)


def from_behind(value, axis, steps):
    count = lax.axis_size(axis)
    initial, last = (max(0, -steps), min(count, count - steps))
    return lax.ppermute(value, axis, [(source, source + steps) for source in range(initial, last)])


def swap(value, axis, mask):
    count = lax.axis_size(axis)
    return lax.ppermute(value, axis, [(source, source ^ mask) for source in range(count)])


def here():
    return lax.axis_index("tm")


def column_shift(block, cols, shift):
    if shift:
        col = lax.broadcasted_iota(jnp.int32, block.shape, 1) % cols
        inside = (col + shift >= 0) & (col + shift < cols)
        block = jnp.where(inside, block, 0.0)
    return block.astype(BF16)


def row_shift(flat, span, shift):
    edge = jnp.zeros((span, flat.shape[1]), flat.dtype)
    if shift < 0:
        return jnp.concatenate([edge, flat[:-span]], axis=0)
    if shift > 0:
        return jnp.concatenate([flat[span:], edge], axis=0)
    return flat


def project_kernel(
    cot_hbm, up_hbm, frames_hbm, w_hbm, flat, hidden_grad, frames_vmem, w_vmem, cot, up, wide, sems
):
    copies = [
        pltpu.make_async_copy(source, target, sems.at[n])
        for n, (source, target) in enumerate(
            [(cot_hbm, cot), (up_hbm, up), (frames_hbm, frames_vmem), (w_hbm, w_vmem)]
        )
    ]
    for copy in copies:
        copy.start()
    slots, frames, own, cols, _ = cot.shape
    copies[0].wait()
    for s in range(slots):
        for q in range(own):
            for t in range(frames):
                base = ((s * own + q) * frames + t) * cols
                wide[base : base + cols, :] = cot[s, t, q].astype(F32)
    g = wide[...].astype(BF16)
    flat[...] = g
    copies[1].wait()
    value = lax.dot_general(g, up[...], NT, preferred_element_type=F32).astype(BF16)
    hidden_grad[...] = value.reshape(hidden_grad.shape)
    copies[2].wait()
    copies[3].wait()


def project(cot, up, frames, weight):
    slots, count, own, cols, width = cot.shape
    places = slots * count * own * cols
    return pl.pallas_call(
        project_kernel,
        out_shape=(
            struct((places, width), BF16),
            struct((slots, places // slots, up.shape[0]), BF16),
            struct(frames.shape, BF16),
            struct(weight.shape, BF16),
        ),
        in_specs=[IN_HBM] * 4,
        out_specs=(IN_VMEM,) * 4,
        scratch_shapes=[
            pltpu.VMEM(cot.shape, BF16),
            pltpu.VMEM(up.shape, BF16),
            pltpu.VMEM((places, width), F32),
            pltpu.SemaphoreType.DMA((4,)),
        ],
        name="project",
        compiler_params=limit(12),
    )(*[pltpu.with_memory_space_constraint(v, pltpu.HBM) for v in (cot, up, frames, weight)])


def forward_kernel(earlier, frames_ref, weight, hidden_grad, slope, keep, send, field, hidden):
    frames, rows, cols, chans = frames_ref.shape
    span = frames * cols
    first = here() == 0
    for r in range(rows):
        for t in range(frames + 2):
            if t < 2:
                value = jnp.where(first, frames_ref[0, r], earlier[frames - 2 + t, r])
            else:
                value = frames_ref[t - 2, r]
            field[r, 8 + t * cols : 8 + (t + 1) * cols, :] = value.astype(F32)
    total = jnp.zeros((rows * span, chans), F32)
    for a in range(3):
        flats = []
        for c in range(3):
            start = 8 + a * cols + c - 1
            block = column_shift(field[:, start : start + span, :], cols, c - 1)
            flats.append(block.reshape(rows * span, chans))
        left = jnp.concatenate(
            [row_shift(flats[c], span, b - 1) for b in range(3) for c in range(3)], axis=1
        )
        right = weight[9 * a : 9 * a + 9].reshape(9 * chans, chans)
        total += jnp.dot(left, right, preferred_element_type=F32)
    sigma = 1.0 / (1.0 + jnp.exp(-total))
    hidden[...] = (total * sigma).astype(BF16).reshape(hidden.shape)
    slope[...] = sigma * (1.0 + total * (1.0 - sigma))
    mine = here() % 2
    for m in range(keep.shape[0]):
        kept, sent = 2 * m + mine, 2 * m + 1 - mine
        keep[m, 0] = hidden[kept]
        keep[m, 1] = hidden_grad[kept]
        send[m, 0] = hidden[sent]
        send[m, 1] = hidden_grad[sent]


def forward(earlier, frames, weight, hidden_grad):
    count, rows, cols, chans = frames.shape
    slots, block, _ = hidden_grad.shape
    length = -(-((count + 2) * cols + 9) // 8) * 8
    return pl.pallas_call(
        forward_kernel,
        out_shape=(struct((slots * block, chans), F32),)
        + (struct((slots // 2, 2, block, chans), BF16),) * 2,
        in_specs=[IN_VMEM] * 4,
        out_specs=(IN_VMEM,) * 3,
        scratch_shapes=[
            pltpu.VMEM((rows, length, chans), F32),
            pltpu.VMEM((slots, block, chans), BF16),
        ],
        name="forward_conv",
        compiler_params=limit(8),
    )(earlier, frames, weight, hidden_grad)


def route_kernel(keep, got, own, *sends):
    me = here() // 2
    mine = here() % 2
    for k, ref in enumerate((own,) + sends):
        ref[mine] = keep[me ^ k]
        ref[1 - mine] = got[me ^ k]


def route(keep, got):
    return pl.pallas_call(
        route_kernel,
        out_shape=(struct((2,) + keep.shape[1:], BF16),) * keep.shape[0],
        in_specs=[IN_VMEM] * 2,
        out_specs=(IN_VMEM,) * keep.shape[0],
        name="route",
        compiler_params=limit(4),
    )(keep, got)


def middle_kernel(size, count, g, slope, *refs):
    got = refs[:count]
    pre_grad, head, keep, send, hidden, hidden_grad, term = refs[count:]
    me = here() // 2
    for k in range(count):
        for c in range(2):
            place = 2 * (me ^ k) + c
            hidden[place] = got[k][c, 0]
            hidden_grad[place] = got[k][c, 1]
    places, chans = slope.shape
    value = hidden_grad[...].reshape(places, chans).astype(F32) * slope[...]
    value = value.astype(BF16).reshape(pre_grad.shape)
    pre_grad[...] = value
    head[...] = value[:, : head.shape[1], :]
    left = hidden[...].reshape(places, chans)
    term[...] = lax.dot_general(left, g[...], TN, preferred_element_type=F32)
    parts, half, lanes = keep.shape
    mine = here() % 2
    for m in range(half // size):
        kept = pl.ds(pl.multiple_of((2 * m + mine) * size, size), size)
        sent = pl.ds(pl.multiple_of((2 * m + 1 - mine) * size, size), size)
        for n in range(parts):
            cut = slice(n * lanes, (n + 1) * lanes)
            keep[n, m * size : (m + 1) * size, :] = term[kept, cut]
            send[n, m * size : (m + 1) * size, :] = term[sent, cut].astype(BF16)


def middle(g, slope, got, shape, size, parts):
    frames, rows, cols, chans = shape
    width = g.shape[1]
    slots, block = 2 * len(got), got[0].shape[2]
    return pl.pallas_call(
        functools.partial(middle_kernel, size, len(got)),
        out_shape=(
            struct((rows, frames * cols, chans), BF16),
            struct((rows, 2 * cols, chans), BF16),
            struct((parts, chans // 2, width // parts), F32),
            struct((parts, chans // 2, width // parts), BF16),
        ),
        in_specs=[IN_VMEM] * (2 + len(got)),
        out_specs=(IN_VMEM,) * 4,
        scratch_shapes=[
            pltpu.VMEM((slots, block, chans), BF16),
            pltpu.VMEM((slots, block, chans), BF16),
            pltpu.VMEM((chans, width), F32),
        ],
        name="middle",
        compiler_params=limit(8),
    )(g, slope, *got)


def backward_kernel(pre_grad, later, weight, out, field):
    frames, rows, cols, chans = out.shape
    span = frames * cols
    field[:, 8 : 8 + span, :] = pre_grad[...].astype(F32)
    field[:, 8 + span : 8 + span + 2 * cols, :] = later[...].astype(F32)
    sums = []
    for a in range(3):
        size = (frames + 2 - a) * cols
        size = -(-size // 16) * 16
        total = jnp.zeros((rows * size, chans), F32)
        flats = []
        for c in range(3):
            start = 8 + 1 - c
            block = column_shift(field[:, start : start + size, :], cols, 1 - c)
            flats.append(block.reshape(rows * size, chans))
        for b in range(3):
            for c in range(3):
                left = row_shift(flats[c], size, 1 - b)
                total += lax.dot_general(
                    left, weight[9 * a + 3 * b + c], NT, preferred_element_type=F32
                )
        sums.append(total.reshape(rows, size, chans))
    edge = sums[0][:, :cols] + sums[0][:, cols : 2 * cols] + sums[1][:, :cols]
    edge = jnp.where(here() == 0, edge, 0.0)
    for t in range(frames):
        at = [slice((t + 2 - a) * cols, (t + 3 - a) * cols) for a in range(3)]
        frame = sums[0][:, at[0]] + sums[1][:, at[1]] + sums[2][:, at[2]]
        if t == 0:
            frame = frame + edge
        out[t] = frame.astype(BF16)


def backward(pre_grad, later, weight, shape):
    count, rows, cols, chans = shape
    length = 8 + -(-(count + 2) * cols // 16) * 16 + 8
    return pl.pallas_call(
        backward_kernel,
        out_shape=struct(shape, BF16),
        in_specs=[IN_VMEM] * 3,
        out_specs=IN_VMEM,
        scratch_shapes=[pltpu.VMEM((rows, length, chans), F32)],
        name="backward_conv",
        compiler_params=limit(8),
    )(pre_grad, later, weight)


def split_kernel(keep, got, mine, *sends):
    me = lax.axis_index(("dp", "rep"))
    mine[...] = keep[me] + got[me].astype(F32)
    for k, send in enumerate(sends, 1):
        send[...] = (keep[me ^ k] + got[me ^ k].astype(F32)).astype(BF16)


def split(keep, got):
    parts, half, width = keep.shape
    return pl.pallas_call(
        split_kernel,
        out_shape=(struct((half, width), F32),) + (struct((half, width), BF16),) * (parts - 1),
        in_specs=[IN_VMEM] * 2,
        out_specs=(IN_VMEM,) * parts,
        name="split_cols",
        compiler_params=limit(4),
    )(keep, got)


def spread_kernel(size, received, mine, *refs):
    got, kept, sends = refs[:received], refs[received], refs[received + 1 :]

    def total(block):
        rows = pl.ds(pl.multiple_of(block * size, size), size)
        value = mine[rows, :]
        for ref in got:
            value = value + ref[rows, :].astype(F32)
        return value

    me = here() // 2
    kept[...] = total(me)
    for k, send in enumerate(sends, 1):
        send[...] = total(me ^ k).astype(BF16)


def spread(mine, got, size):
    half, width = mine.shape
    count = half // size
    return pl.pallas_call(
        functools.partial(spread_kernel, size, len(got)),
        out_shape=(struct((size, width), F32),) + (struct((size, width), BF16),) * (count - 1),
        in_specs=[IN_VMEM] * (1 + len(got)),
        out_specs=(IN_VMEM,) * count,
        name="split_rows",
        compiler_params=limit(4),
    )(mine, *got)


def final_kernel(factor, mine, *refs):
    value = mine[...]
    for ref in refs[:-1]:
        value = value + ref[...].astype(F32)
    refs[-1][...] = value * factor


def final(mine, got, factor):
    return pl.pallas_call(
        functools.partial(final_kernel, factor),
        out_shape=struct(mine.shape, F32),
        in_specs=[IN_VMEM] * (1 + len(got)),
        out_specs=IN_VMEM,
        name="final_sum",
        compiler_params=limit(4),
    )(mine, *got)


def local(clip_frames, conv_weight, up_weight, cotangent):
    frames_local = clip_frames[0]
    frames, rows, cols, chans = frames_local.shape
    width = up_weight.shape[1]
    time_count = lax.axis_size("tm")
    clip_count = lax.axis_size(("dp", "rep"))
    weight = conv_weight.reshape(27, chans, chans)
    factor = 1.0 / math.sqrt(clip_count * frames * time_count * rows * cols)
    size = chans // time_count

    earlier = from_behind(frames_local, "tm", 1)
    own_rows = rows // time_count
    cot = cotangent.reshape(time_count, frames, own_rows, cols, width)
    flat_g, hidden_grad, near, weight = project(cot, up_weight, frames_local, weight)
    slope, keep, send = forward(earlier, near, weight, hidden_grad)
    got = swap(send, "tm", 1)
    own, *sends = route(keep, got)
    arrived = [swap(sends[k - 1], "tm", 2 * k) for k in range(1, time_count // 2)]
    pre_grad, head, keep, send = middle(
        flat_g, slope, [own] + arrived, frames_local.shape, size, clip_count
    )
    got = swap(send, "tm", 1)
    later = from_behind(head, "tm", -1)
    if clip_count <= DIRECT and time_count // 2 <= DIRECT:
        mine, *sends = split(keep, got)
        arrived = [swap(sends[k - 1], ("dp", "rep"), k) for k in range(1, clip_count)]
        kept, *sends = spread(mine, arrived, size)
        arrived = [swap(sends[k - 1], "tm", 2 * k) for k in range(1, time_count // 2)]
        summed = final(kept, arrived, factor)
    else:
        value = keep + got.astype(F32)
        value = lax.psum_scatter(value, ("dp", "rep"), scatter_dimension=0, tiled=True)[0]
        pairs = [[s for s in range(time_count) if s % 2 == c] for c in range(2)]
        value = lax.psum_scatter(
            value, "tm", scatter_dimension=0, axis_index_groups=pairs, tiled=True
        )
        summed = value * factor
    input_grad = backward(pre_grad, later, weight, frames_local.shape)
    return (input_grad[None], summed)


def solution(mesh):
    in_specs = (
        P(("dp", "rep"), "tm", None, None, None),
        P(),
        P(),
        P(("dp", "rep"), None, "tm", None, None),
    )
    out_specs = (P(("dp", "rep"), "tm", None, None, None), P("tm", ("dp", "rep")))
    return jax.shard_map(local, mesh=mesh, in_specs=in_specs, out_specs=out_specs, check_vma=False)
```

```python
import functools
import math

import jax
import jax.numpy as jnp
from jax import lax
from jax.experimental import pallas as pl
from jax.experimental.pallas import tpu as pltpu
from jax.sharding import PartitionSpec as P


F32 = jnp.float32
BF16 = jnp.bfloat16
IN_VMEM = pl.BlockSpec(memory_space=pltpu.VMEM)
IN_HBM = pl.BlockSpec(memory_space=pltpu.HBM)
NT = (((1,), (1,)), ((), ()))
TN = (((0,), (0,)), ((), ()))
DIRECT = 4
MIB = 1024 * 1024


def limit(mib):
    return pltpu.CompilerParams(vmem_limit_bytes=mib * MIB)


def struct(shape, dtype):
    return jax.ShapeDtypeStruct(shape, dtype)


def from_behind(value, axis, steps):
    count = lax.axis_size(axis)
    initial, last = (max(0, -steps), min(count, count - steps))
    return lax.ppermute(value, axis, [(source, source + steps) for source in range(initial, last)])


def swap(value, axis, mask):
    count = lax.axis_size(axis)
    return lax.ppermute(value, axis, [(source, source ^ mask) for source in range(count)])


def swaps(values, axis, step):
    arrived = []
    for k, value in enumerate(values, 1):
        arrived.append(swap(value, axis, step * k))
    return arrived


def here():
    return lax.axis_index("tm")


def column_shift(block, cols, shift):
    if shift:
        col = lax.broadcasted_iota(jnp.int32, block.shape, 1) % cols
        inside = (col + shift >= 0) & (col + shift < cols)
        block = jnp.where(inside, block, 0.0)
    return block.astype(BF16)


def row_shift(flat, span, shift):
    edge = jnp.zeros((span, flat.shape[1]), flat.dtype)
    if shift < 0:
        return jnp.concatenate([edge, flat[:-span]], axis=0)
    if shift > 0:
        return jnp.concatenate([flat[span:], edge], axis=0)
    return flat


def project_kernel(
    cot_hbm, up_hbm, frames_hbm, w_hbm, flat, hidden_grad, frames_vmem, w_vmem, cot, up, wide, sems
):
    copies = [
        pltpu.make_async_copy(source, target, sems.at[n])
        for n, (source, target) in enumerate(
            [(cot_hbm, cot), (up_hbm, up), (frames_hbm, frames_vmem), (w_hbm, w_vmem)]
        )
    ]
    for copy in copies:
        copy.start()
    slots, frames, own, cols, _ = cot.shape
    copies[0].wait()
    for s in range(slots):
        for q in range(own):
            for t in range(frames):
                base = ((s * own + q) * frames + t) * cols
                wide[base : base + cols, :] = cot[s, t, q].astype(F32)
    g = wide[...].astype(BF16)
    flat[...] = g
    copies[1].wait()
    value = lax.dot_general(g, up[...], NT, preferred_element_type=F32).astype(BF16)
    hidden_grad[...] = value.reshape(hidden_grad.shape)
    copies[2].wait()
    copies[3].wait()


def project(cot, up, frames, weight):
    slots, count, own, cols, width = cot.shape
    places = slots * count * own * cols
    return pl.pallas_call(
        project_kernel,
        out_shape=(
            struct((places, width), BF16),
            struct((slots, places // slots, up.shape[0]), BF16),
            struct(frames.shape, BF16),
            struct(weight.shape, BF16),
        ),
        in_specs=[IN_HBM] * 4,
        out_specs=(IN_VMEM,) * 4,
        scratch_shapes=[
            pltpu.VMEM(cot.shape, BF16),
            pltpu.VMEM(up.shape, BF16),
            pltpu.VMEM((places, width), F32),
            pltpu.SemaphoreType.DMA((4,)),
        ],
        name="project",
        compiler_params=limit(12),
    )(*[pltpu.with_memory_space_constraint(v, pltpu.HBM) for v in (cot, up, frames, weight)])


def by_parity(chans, size):
    row = lax.broadcasted_iota(jnp.int32, (chans, chans), 0)
    col = lax.broadcasted_iota(jnp.int32, (chans, chans), 1)
    block = row // size
    target = (block % 2) * (chans // 2) + (block // 2) * size + row % size
    return jnp.where(target == col, 1.0, 0.0).astype(BF16)


def forward_kernel(
    size, earlier, frames_ref, weight, hidden_grad, slope, keep, send, field, hidden
):
    frames, rows, cols, chans = frames_ref.shape
    span = frames * cols
    first = here() == 0
    for r in range(rows):
        for t in range(frames + 2):
            if t < 2:
                value = jnp.where(first, frames_ref[0, r], earlier[frames - 2 + t, r])
            else:
                value = frames_ref[t - 2, r]
            field[r, 8 + t * cols : 8 + (t + 1) * cols, :] = value.astype(F32)
    total = jnp.zeros((rows * span, chans), F32)
    for a in range(3):
        flats = []
        for c in range(3):
            start = 8 + a * cols + c - 1
            block = column_shift(field[:, start : start + span, :], cols, c - 1)
            flats.append(block.reshape(rows * span, chans))
        left = jnp.concatenate(
            [row_shift(flats[c], span, b - 1) for b in range(3) for c in range(3)], axis=1
        )
        right = weight[9 * a : 9 * a + 9].reshape(9 * chans, chans)
        total += jnp.dot(left, right, preferred_element_type=F32)
    sigma = 1.0 / (1.0 + jnp.exp(-total))
    ordered = jnp.dot(
        (total * sigma).astype(BF16), by_parity(chans, size), preferred_element_type=F32
    ).astype(BF16)
    half = chans // 2
    for p in range(2):
        hidden[p] = ordered[:, p * half : (p + 1) * half].reshape(hidden.shape[1:])
    slope[...] = sigma * (1.0 + total * (1.0 - sigma))
    mine = here() % 2
    block = hidden_grad.shape[1]
    for part, core in ((keep, mine), (send, 1 - mine)):
        for m in range(part.shape[0]):
            part[m, 0] = hidden[core, m]
            part[m, 1, :block] = hidden_grad[2 * m + core, :, :half]
            part[m, 1, block:] = hidden_grad[2 * m + core, :, half:]


def forward(earlier, frames, weight, hidden_grad, size):
    count, rows, cols, chans = frames.shape
    slots, block, _ = hidden_grad.shape
    length = -(-((count + 2) * cols + 9) // 8) * 8
    return pl.pallas_call(
        functools.partial(forward_kernel, size),
        out_shape=(struct((slots * block, chans), F32),)
        + (struct((slots // 2, 2, 2 * block, chans // 2), BF16),) * 2,
        in_specs=[IN_VMEM] * 4,
        out_specs=(IN_VMEM,) * 3,
        scratch_shapes=[
            pltpu.VMEM((rows, length, chans), F32),
            pltpu.VMEM((2, slots // 2, 2 * block, chans // 2), BF16),
        ],
        name="forward_conv",
        compiler_params=limit(8),
    )(earlier, frames, weight, hidden_grad)


def route_kernel(keep, got, own, *sends):
    me = here() // 2
    mine = here() % 2
    for k, ref in enumerate((own,) + sends):
        ref[mine] = keep[me ^ k]
        ref[1 - mine] = got[me ^ k]


def route(keep, got):
    return pl.pallas_call(
        route_kernel,
        out_shape=(struct((2,) + keep.shape[1:], BF16),) * keep.shape[0],
        in_specs=[IN_VMEM] * 2,
        out_specs=(IN_VMEM,) * keep.shape[0],
        name="route",
        compiler_params=limit(4),
    )(keep, got)


def middle_kernel(count, direct, g, other, slope, *refs):
    got = refs[:count]
    pre_grad, *outs, hidden, hidden_grad, term = refs[count:]
    me = here() // 2
    mine = here() % 2
    places, chans = slope.shape
    block, half = hidden.shape[2:]
    for k in range(count):
        for c in range(2):
            place = 2 * (me ^ k) + c
            hidden[0, place] = got[k][c, 0, :block]
            hidden[1, place] = got[k][c, 0, block:]
            hidden_grad[place, :, :half] = got[k][c, 1, :block]
            hidden_grad[place, :, half:] = got[k][c, 1, block:]
    value = hidden_grad[...].reshape(places, chans).astype(F32) * slope[...]
    pre_grad[...] = value.astype(BF16).reshape(pre_grad.shape)
    total = lax.dot_general(
        hidden[mine].reshape(places, half), g[...], TN, preferred_element_type=F32
    ) + lax.dot_general(
        hidden[1 - mine].reshape(places, half), other[...], TN, preferred_element_type=F32
    )
    parts, _, lanes = term.shape
    for n in range(parts):
        term[n] = total[:, n * lanes : (n + 1) * lanes]
    if direct:
        spot = lax.axis_index(("dp", "rep"))
        outs[0][...] = term[spot]
        for k in range(1, parts):
            outs[k][...] = term[spot ^ k].astype(BF16)
    else:
        outs[0][...] = term[...]


def middle(g, other, slope, got, shape, parts, direct):
    frames, rows, cols, chans = shape
    lanes = g.shape[1] // parts
    half = chans // 2
    slots, block = 2 * len(got), got[0].shape[2] // 2
    if direct:
        outs = (struct((half, lanes), F32),) + (struct((half, lanes), BF16),) * (parts - 1)
    else:
        outs = (struct((parts, half, lanes), F32),)
    return pl.pallas_call(
        functools.partial(middle_kernel, len(got), direct),
        out_shape=(struct((rows, frames * cols, chans), BF16),) + outs,
        in_specs=[IN_VMEM] * (3 + len(got)),
        out_specs=(IN_VMEM,) * (1 + len(outs)),
        scratch_shapes=[
            pltpu.VMEM((2, slots, block, half), BF16),
            pltpu.VMEM((slots, block, chans), BF16),
            pltpu.VMEM((parts, half, lanes), F32),
        ],
        name="middle",
        compiler_params=limit(8),
    )(g, other, slope, *got)


def backward_kernel(frames, cols, pre_grad, weight, own, previous, field):
    rows, span, chans = pre_grad.shape
    field[:, 8 : 8 + span, :] = pre_grad[...].astype(F32)
    sums = [jnp.zeros((rows * span, chans), F32)] * 3
    for c in range(3):
        start = 8 + 1 - c
        block = column_shift(field[:, start : start + span, :], cols, 1 - c)
        flat = block.reshape(rows * span, chans)
        for b in range(3):
            left = row_shift(flat, span, 1 - b)
            for a in range(3):
                sums[a] += lax.dot_general(
                    left, weight[9 * a + 3 * b + c], NT, preferred_element_type=F32
                )
    sums = [value.reshape(rows, span, chans) for value in sums]

    def at(a, t):
        return sums[a][:, t * cols : (t + 1) * cols]

    before = [at(0, 0), at(0, 1) + at(1, 0)]
    for t in range(2):
        previous[:, t * cols : (t + 1) * cols, :] = before[t].astype(BF16)
    edge = jnp.where(here() == 0, before[0] + before[1], 0.0)
    for t in range(frames):
        value = at(2, t)
        if t + 1 < frames:
            value = value + at(1, t + 1)
        if t + 2 < frames:
            value = value + at(0, t + 2)
        if t == 0:
            value = value + edge
        own[:, t * cols : (t + 1) * cols, :] = value


def backward(pre_grad, weight, frames, cols):
    rows, span, chans = pre_grad.shape
    return pl.pallas_call(
        functools.partial(backward_kernel, frames, cols),
        out_shape=(struct((rows, span, chans), F32), struct((rows, 2 * cols, chans), BF16)),
        in_specs=[IN_VMEM] * 2,
        out_specs=(IN_VMEM,) * 2,
        scratch_shapes=[pltpu.VMEM((rows, 8 + span + 8, chans), F32)],
        name="backward_conv",
        compiler_params=limit(8),
    )(pre_grad, weight)


def finish_kernel(own, later, out):
    frames, _, cols, _ = out.shape
    for t in range(frames):
        value = own[:, t * cols : (t + 1) * cols, :]
        if t >= frames - 2:
            first = (t - frames + 2) * cols
            value = value + later[:, first : first + cols, :].astype(F32)
        out[t] = value.astype(BF16)


def finish(own, later, shape):
    return pl.pallas_call(
        finish_kernel,
        out_shape=struct(shape, BF16),
        in_specs=[IN_VMEM] * 2,
        out_specs=IN_VMEM,
        name="finish",
        compiler_params=limit(4),
    )(own, later)


def spread_kernel(size, received, mine, *refs):
    got, kept, sends = refs[:received], refs[received], refs[received + 1 :]

    def total(block):
        rows = pl.ds(pl.multiple_of(block * size, size), size)
        value = mine[rows, :]
        for ref in got:
            value = value + ref[rows, :].astype(F32)
        return value

    me = here() // 2
    kept[...] = total(me)
    for k, send in enumerate(sends, 1):
        send[...] = total(me ^ k).astype(BF16)


def spread(mine, got, size):
    half, width = mine.shape
    count = half // size
    return pl.pallas_call(
        functools.partial(spread_kernel, size, len(got)),
        out_shape=(struct((size, width), F32),) + (struct((size, width), BF16),) * (count - 1),
        in_specs=[IN_VMEM] * (1 + len(got)),
        out_specs=(IN_VMEM,) * count,
        name="split_rows",
        compiler_params=limit(4),
    )(mine, *got)


def final_kernel(factor, mine, *refs):
    value = mine[...]
    for ref in refs[:-1]:
        value = value + ref[...].astype(F32)
    refs[-1][...] = value * factor


def final(mine, got, factor):
    return pl.pallas_call(
        functools.partial(final_kernel, factor),
        out_shape=struct(mine.shape, F32),
        in_specs=[IN_VMEM] * (1 + len(got)),
        out_specs=IN_VMEM,
        name="final_sum",
        compiler_params=limit(4),
    )(mine, *got)


def whole(clip_frames, conv_weight, up_weight, cotangent):
    frames_local = clip_frames[0]
    frames, rows, cols, chans = frames_local.shape
    width = up_weight.shape[1]
    time_count = lax.axis_size("tm")
    clip_count = lax.axis_size(("dp", "rep"))
    weight = conv_weight.reshape(27, chans, chans)
    factor = 1.0 / math.sqrt(clip_count * frames * time_count * rows * cols)
    size = chans // time_count

    earlier = from_behind(frames_local, "tm", 1)
    own_rows = rows // time_count
    cot = cotangent.reshape(time_count, frames, own_rows, cols, width)
    direct = clip_count <= DIRECT and time_count // 2 <= DIRECT
    flat_g, hidden_grad, near, weight = project(cot, up_weight, frames_local, weight)
    other_g = swap(flat_g, "tm", 1)
    slope, keep, send = forward(earlier, near, weight, hidden_grad, size)
    got = swap(send, "tm", 1)
    own, *sends = route(keep, got)
    arrived = swaps(sends, "tm", 2)
    pre_grad, mine, *sends = middle(
        flat_g, other_g, slope, [own] + arrived, frames_local.shape, clip_count, direct
    )
    if direct:
        arrived = swaps(sends, ("dp", "rep"), 1)
        kept, *sends = spread(mine, arrived, size)
        arrived = swaps(sends, "tm", 2)
        summed = final(kept, arrived, factor)
    else:
        value = lax.psum_scatter(mine, ("dp", "rep"), scatter_dimension=0, tiled=True)[0]
        pairs = [[s for s in range(time_count) if s % 2 == c] for c in range(2)]
        value = lax.psum_scatter(
            value, "tm", scatter_dimension=0, axis_index_groups=pairs, tiled=True
        )
        summed = value * factor
    partial, previous = backward(pre_grad, weight, frames, cols)
    later = from_behind(previous, "tm", -1)
    input_grad = finish(partial, later, frames_local.shape)
    return (input_grad[None], summed)


def solution(mesh):
    in_specs = (
        P(("dp", "rep"), "tm", None, None, None),
        P(),
        P(),
        P(("dp", "rep"), None, "tm", None, None),
    )
    out_specs = (P(("dp", "rep"), "tm", None, None, None), P("tm", ("dp", "rep")))
    return jax.shard_map(whole, mesh=mesh, in_specs=in_specs, out_specs=out_specs, check_vma=False)
```

```python
import functools
import math

import jax
import jax.numpy as jnp
from jax import lax
from jax.experimental import pallas as pl
from jax.experimental.pallas import tpu as pltpu
from jax.sharding import PartitionSpec as P


F32 = jnp.float32
BF16 = jnp.bfloat16
IN_VMEM = pl.BlockSpec(memory_space=pltpu.VMEM)
IN_HBM = pl.BlockSpec(memory_space=pltpu.HBM)
NT = (((1,), (1,)), ((), ()))
TN = (((0,), (0,)), ((), ()))
DIRECT = 4
MIB = 1024 * 1024


def limit(mib):
    return pltpu.CompilerParams(vmem_limit_bytes=mib * MIB)


def struct(shape, dtype):
    return jax.ShapeDtypeStruct(shape, dtype)


def in_hbm(*values):
    return [pltpu.with_memory_space_constraint(value, pltpu.HBM) for value in values]


def up_to(value, step):
    return -(-value // step) * step


def swap(value, axis, mask):
    count = lax.axis_size(axis)
    return lax.ppermute(value, axis, [(source, source ^ mask) for source in range(count)])


def swaps(values, axis, step):
    arrived = []
    for k, value in enumerate(values, 1):
        arrived.append(swap(value, axis, step * k))
    return arrived


def here():
    return lax.axis_index("tm")


def column_shift(block, cols, shift):
    if shift:
        col = lax.broadcasted_iota(jnp.int32, block.shape, 1) % cols
        inside = (col + shift >= 0) & (col + shift < cols)
        block = jnp.where(inside, block, 0.0)
    return block.astype(BF16)


def row_shift(flat, span, shift):
    edge = jnp.zeros((span, flat.shape[1]), flat.dtype)
    if shift < 0:
        return jnp.concatenate([edge, flat[:-span]], axis=0)
    if shift > 0:
        return jnp.concatenate([flat[span:], edge], axis=0)
    return flat


def pack_kernel(near, frames_hbm, *refs):
    parts, (frames_vmem, wide, sem) = refs[:-3], refs[-3:]
    copy = pltpu.make_async_copy(frames_hbm, frames_vmem, sem)
    copy.start()
    frames, rows, cols, chans = frames_vmem.shape
    edge = jnp.zeros((frames * cols, chans), F32)
    wide[0] = edge
    wide[rows + 1] = edge
    copy.wait()
    for r in range(rows):
        for t in range(frames):
            wide[r + 1, t * cols : (t + 1) * cols, :] = frames_vmem[t, r].astype(F32)
    me = here() // 2
    for k, part in enumerate(parts):
        part[...] = wide[pl.ds((me ^ k) * near, near + 2)].astype(BF16)


def pack(frames, near, chips):
    count, rows, cols, chans = frames.shape
    return pl.pallas_call(
        functools.partial(pack_kernel, near),
        out_shape=(struct((near + 2, count * cols, chans), BF16),) * chips,
        in_specs=[IN_HBM],
        out_specs=(IN_VMEM,) * chips,
        scratch_shapes=[
            pltpu.VMEM(frames.shape, BF16),
            pltpu.VMEM((rows + 2, count * cols, chans), F32),
            pltpu.SemaphoreType.DMA(()),
        ],
        name="pack",
        compiler_params=limit(8),
        cost_estimate=pl.CostEstimate(flops=20_000_000_000, transcendentals=0, bytes_accessed=2 * frames.size),
    )(*in_hbm(frames))


def project_kernel(cot_hbm, up_hbm, mate, g, hidden_grad, cot, up, wide, sems):
    copies = [
        pltpu.make_async_copy(cot_hbm, cot, sems.at[0]),
        pltpu.make_async_copy(up_hbm, up, sems.at[1]),
    ]
    for copy in copies:
        copy.start()
    slots, frames, own, cols, _ = cot.shape
    mine = here() % 2
    for source, core in ((mate, 1 - mine), (cot, mine)):
        if source is cot:
            copies[0].wait()
        for s in range(slots):
            for t in range(frames):
                for q in range(own):
                    base = (s * frames + t) * cols
                    wide[core, q, base : base + cols, :] = source[s, t, q].astype(F32)
    value = wide[...].reshape(g.shape).astype(BF16)
    g[...] = value
    copies[1].wait()
    hidden_grad[...] = lax.dot_general(value, up[...], NT, preferred_element_type=F32).astype(BF16)


def project(cot, up, mate):
    slots, count, own, cols, width = cot.shape
    places = 2 * slots * count * own * cols
    return pl.pallas_call(
        project_kernel,
        out_shape=(struct((places, width), BF16), struct((places, up.shape[0]), BF16)),
        in_specs=[IN_HBM, IN_HBM, IN_VMEM],
        out_specs=(IN_VMEM,) * 2,
        scratch_shapes=[
            pltpu.VMEM(cot.shape, BF16),
            pltpu.VMEM(up.shape, BF16),
            pltpu.VMEM((2, own, slots * count * cols, width), F32),
            pltpu.SemaphoreType.DMA((2,)),
        ],
        name="project",
        compiler_params=limit(16),
    )(*in_hbm(cot, up), mate)


def gather_kernel(*refs):
    parts, out = refs[:-1], refs[-1]
    me = here() // 2
    for k, part in enumerate(parts):
        out[me ^ k] = part[...]


def gather(parts):
    return pl.pallas_call(
        gather_kernel,
        out_shape=struct((len(parts),) + parts[0].shape, BF16),
        in_specs=[IN_VMEM] * len(parts),
        out_specs=IN_VMEM,
        name="gather",
        compiler_params=limit(4),
    )(*parts)


def by_parity(chans, size):
    row = lax.broadcasted_iota(jnp.int32, (chans, chans), 0)
    col = lax.broadcasted_iota(jnp.int32, (chans, chans), 1)
    block = row // size
    target = (block % 2) * (chans // 2) + (block // 2) * size + row % size
    return jnp.where(target == col, 1.0, 0.0).astype(BF16)


def rows_kernel(size, cols, direct, half_ref, other, weight, g, hidden_grad, *refs):
    chips, tall, block, chans = half_ref.shape
    near = tall - 2
    *outs, field, hidden, grads, term = refs
    backs, outs = outs[:chips], outs[chips:]
    length = 2 * chips * block
    base = up_to(2 * cols + 1, 8)
    me = here() // 2
    mine = here() % 2
    for source, core in ((half_ref, mine), (other, 1 - mine)):
        for z in range(chips):
            start = pl.multiple_of(base + (2 * z + core) * block, 8)
            for i in range(tall):
                field[i, pl.ds(start, block), :] = source[z, i].astype(F32)
    for t in range(1, 3):
        field[:, base - t * cols : base - (t - 1) * cols, :] = field[:, base : base + cols, :]
    total = jnp.zeros((near * length, chans), F32)
    for a in range(3):
        flats = []
        for c in range(3):
            start = base + (a - 2) * cols + c - 1
            flats.append(column_shift(field[:, start : start + length, :], cols, c - 1))
        left = jnp.concatenate(
            [
                flats[c][b : b + near].reshape(near * length, chans)
                for b in range(3)
                for c in range(3)
            ],
            axis=1,
        )
        right = weight[9 * a : 9 * a + 9].reshape(9 * chans, chans)
        total += jnp.dot(left, right, preferred_element_type=F32)
    sigma = 1.0 / (1.0 + jnp.exp(-total))
    ordered = jnp.dot(
        (total * sigma).astype(BF16), by_parity(chans, size), preferred_element_type=F32
    ).astype(BF16)
    half = chans // 2
    for p in range(2):
        hidden[p] = ordered[:, p * half : (p + 1) * half]
    product = lax.dot_general(hidden[mine], g[...], TN, preferred_element_type=F32)
    parts, _, lanes = term.shape
    for n in range(parts):
        term[n] = product[:, n * lanes : (n + 1) * lanes]
    if direct:
        spot = lax.axis_index(("dp", "rep"))
        outs[0][...] = term[spot]
        for k in range(1, parts):
            outs[k][...] = term[spot ^ k].astype(BF16)
    else:
        outs[0][...] = term[...]
    slope = sigma * (1.0 + total * (1.0 - sigma))
    value = (hidden_grad[...].astype(F32) * slope).astype(BF16).astype(F32)
    grads[:, :length, :] = value.reshape(near, length, chans)
    grads[:, length:, :] = jnp.zeros((near, grads.shape[1] - length, chans), F32)
    for k, back in enumerate(backs):
        start = pl.multiple_of((2 * (me ^ k) + mine) * block, 8)
        back[...] = grads[:, pl.ds(start, back.shape[1]), :].astype(BF16)


def rows_of(half_ref, other, weight, g, hidden_grad, size, cols, parts, direct):
    chips, tall, block, chans = half_ref.shape
    near = tall - 2
    length = 2 * chips * block
    lanes = g.shape[1] // parts
    half = chans // 2
    reach = block + 2 * cols
    if direct:
        outs = (struct((half, lanes), F32),) + (struct((half, lanes), BF16),) * (parts - 1)
    else:
        outs = (struct((parts, half, lanes), F32),)
    outs = (struct((near, reach, chans), BF16),) * chips + outs
    return pl.pallas_call(
        functools.partial(rows_kernel, size, cols, direct),
        out_shape=outs,
        in_specs=[IN_VMEM] * 5,
        out_specs=(IN_VMEM,) * len(outs),
        scratch_shapes=[
            pltpu.VMEM((tall, up_to(up_to(2 * cols + 1, 8) + length + 1, 8), chans), F32),
            pltpu.VMEM((2, near * length, half), BF16),
            pltpu.VMEM((near, up_to(length + 2 * cols, 8), chans), F32),
            pltpu.VMEM((parts, half, lanes), F32),
        ],
        name="rows",
        compiler_params=limit(32),
    )(half_ref, other, weight, g, hidden_grad)


def spread_kernel(size, received, mine, *refs):
    got, refs = refs[:received], refs[received:]
    chips = (len(refs) + 1) // 2
    backs, kept, sends = refs[: chips - 1], refs[chips - 1], refs[chips:]

    def total(block):
        rows = pl.ds(pl.multiple_of(block * size, size), size)
        value = mine[rows, :]
        for ref in got:
            value = value + ref[rows, :].astype(F32)
        return value

    me = here() // 2
    kept[...] = total(me)
    for k, (back, send) in enumerate(zip(backs, sends), 1):
        send[:size] = total(me ^ k).astype(BF16)
        near, reach, _ = back.shape
        for i in range(near):
            send[size + i * reach : size + (i + 1) * reach] = back[i]


def spread(mine, got, backs, size):
    half, width = mine.shape
    chips = half // size
    near, reach, _ = backs[0].shape
    send = struct((size + near * reach, width), BF16)
    return pl.pallas_call(
        functools.partial(spread_kernel, size, len(got)),
        out_shape=(struct((size, width), F32),) + (send,) * (chips - 1),
        in_specs=[IN_VMEM] * (1 + len(got) + len(backs)),
        out_specs=(IN_VMEM,) * chips,
        name="split_rows",
        compiler_params=limit(4),
    )(mine, *got, *backs)


def finish_kernel(size, factor, kept, weight, own, *refs):
    got, (summed, out, field) = refs[:-3], refs[-3:]
    frames, rows, cols, chans = out.shape
    near, reach, _ = own.shape
    me = here() // 2
    value = kept[...]
    for ref in got:
        value = value + ref[:size].astype(F32)
    summed[...] = value * factor
    for i in range(near):
        field[me * near + i, 8 : 8 + reach, :] = own[i].astype(F32)
        for k, ref in enumerate(got, 1):
            first = size + i * reach
            field[(me ^ k) * near + i, 8 : 8 + reach, :] = ref[first : first + reach].astype(F32)
    span = up_to(reach, 16)
    sums = [jnp.zeros((rows * span, chans), F32)] * 3
    for c in range(3):
        block = column_shift(field[:, 9 - c : 9 - c + span, :], cols, 1 - c)
        flat = block.reshape(rows * span, chans)
        for b in range(3):
            left = row_shift(flat, span, 1 - b)
            for a in range(3):
                sums[a] += lax.dot_general(
                    left, weight[9 * a + 3 * b + c], NT, preferred_element_type=F32
                )
    sums = [value.reshape(rows, span, chans) for value in sums]

    def at(a, t):
        return sums[a][:, t * cols : (t + 1) * cols]

    edge = jnp.where(here() == 0, at(0, 0) + at(0, 1) + at(1, 0), 0.0)
    for t in range(frames):
        value = at(0, t + 2) + at(1, t + 1) + at(2, t)
        if t == 0:
            value = value + edge
        out[t] = value.astype(BF16)


def finish(kept, weight, own, got, shape, size, factor):
    _, rows, _, chans = shape
    reach = own.shape[1]
    return pl.pallas_call(
        functools.partial(finish_kernel, size, factor),
        out_shape=(struct(kept.shape, F32), struct(shape, BF16)),
        in_specs=[IN_VMEM] * (3 + len(got)),
        out_specs=(IN_VMEM,) * 2,
        scratch_shapes=[pltpu.VMEM((rows, 16 + up_to(reach, 16), chans), F32)],
        name="finish",
        compiler_params=limit(16),
    )(kept, weight, own, *got)


def whole(clip_frames, conv_weight, up_weight, cotangent):
    frames_local = clip_frames[0]
    frames, rows, cols, chans = frames_local.shape
    width = up_weight.shape[1]
    time_count = lax.axis_size("tm")
    clip_count = lax.axis_size(("dp", "rep"))
    weight = conv_weight.reshape(27, chans, chans)
    factor = 1.0 / math.sqrt(clip_count * frames * time_count * rows * cols)
    size = chans // time_count
    chips = time_count // 2
    own_rows = rows // time_count
    direct = clip_count <= DIRECT and chips <= DIRECT and width == clip_count * chans

    cot = cotangent.reshape(time_count, frames, own_rows, cols, width)
    mate = swap(cot, "tm", 1)
    parts = pack(frames_local, 2 * own_rows, chips)
    arrived = swaps(parts[1:], "tm", 2)
    half = gather([parts[0]] + arrived)
    other = swap(half, "tm", 1)
    g, hidden_grad = project(cot, up_weight, mate)
    outs = rows_of(half, other, weight, g, hidden_grad, size, cols, clip_count, direct)
    (own, *backs), (mine, *sends) = outs[:chips], outs[chips:]
    if direct:
        arrived = swaps(sends, ("dp", "rep"), 1)
        kept, *sends = spread(mine, arrived, backs, size)
    else:
        value = lax.psum_scatter(mine, ("dp", "rep"), scatter_dimension=0, tiled=True)[0]
        pairs = [[s for s in range(time_count) if s % 2 == c] for c in range(2)]
        kept = lax.psum_scatter(
            value, "tm", scatter_dimension=0, axis_index_groups=pairs, tiled=True
        )
        empty = jnp.zeros((size, chans), BF16)
        sends = [jnp.concatenate([empty, back.reshape(-1, chans)], axis=0) for back in backs]
    arrived = swaps(sends, "tm", 2)
    if not direct:
        summed = kept * factor
        kept = jnp.zeros((size, chans), F32)
        input_grad = finish(kept, weight, own, arrived, frames_local.shape, size, factor)[1]
        return (input_grad[None], summed)
    summed, input_grad = finish(kept, weight, own, arrived, frames_local.shape, size, factor)
    return (input_grad[None], summed)


def solution(mesh):
    in_specs = (
        P(("dp", "rep"), "tm", None, None, None),
        P(),
        P(),
        P(("dp", "rep"), None, "tm", None, None),
    )
    out_specs = (P(("dp", "rep"), "tm", None, None, None), P("tm", ("dp", "rep")))
    return jax.shard_map(whole, mesh=mesh, in_specs=in_specs, out_specs=out_specs, check_vma=False)
```

```python
import functools
import math

import jax
import jax.numpy as jnp
from jax import lax
from jax.experimental import pallas as pl
from jax.experimental.pallas import tpu as pltpu
from jax.sharding import PartitionSpec as P


F32 = jnp.float32
BF16 = jnp.bfloat16
IN_VMEM = pl.BlockSpec(memory_space=pltpu.VMEM)
IN_HBM = pl.BlockSpec(memory_space=pltpu.HBM)
NT = (((1,), (1,)), ((), ()))
TN = (((0,), (0,)), ((), ()))
DIRECT = 4
MIB = 1024 * 1024


def limit(mib):
    return pltpu.CompilerParams(vmem_limit_bytes=mib * MIB)


def struct(shape, dtype):
    return jax.ShapeDtypeStruct(shape, dtype)


def in_hbm(*values):
    return [pltpu.with_memory_space_constraint(value, pltpu.HBM) for value in values]


def up_to(value, step):
    return -(-value // step) * step


def swap(value, axis, mask):
    count = lax.axis_size(axis)
    return lax.ppermute(value, axis, [(source, source ^ mask) for source in range(count)])


def swaps(values, axis, step):
    arrived = []
    for k, value in enumerate(values, 1):
        arrived.append(swap(value, axis, step * k))
    return arrived


def here():
    return lax.axis_index("tm")


def column_shift(block, cols, shift):
    if shift:
        col = lax.broadcasted_iota(jnp.int32, block.shape, 1) % cols
        inside = (col + shift >= 0) & (col + shift < cols)
        block = jnp.where(inside, block, 0.0)
    return block.astype(BF16)


def row_shift(flat, span, shift):
    edge = jnp.zeros((span, flat.shape[1]), flat.dtype)
    if shift < 0:
        return jnp.concatenate([edge, flat[:-span]], axis=0)
    if shift > 0:
        return jnp.concatenate([flat[span:], edge], axis=0)
    return flat


def pack_kernel(near, frames_hbm, *refs):
    parts, (frames_vmem, wide, sem) = refs[:-3], refs[-3:]
    copy = pltpu.make_async_copy(frames_hbm, frames_vmem, sem)
    copy.start()
    frames, rows, cols, chans = frames_vmem.shape
    edge = jnp.zeros((frames * cols, chans), F32)
    wide[0] = edge
    wide[rows + 1] = edge
    copy.wait()
    for r in range(rows):
        for t in range(frames):
            wide[r + 1, t * cols : (t + 1) * cols, :] = frames_vmem[t, r].astype(F32)
    me = here() // 2
    for k, part in enumerate(parts):
        part[...] = wide[pl.ds((me ^ k) * near, near + 2)].astype(BF16)


def pack(frames, near, chips):
    count, rows, cols, chans = frames.shape
    return pl.pallas_call(
        functools.partial(pack_kernel, near),
        out_shape=(struct((near + 2, count * cols, chans), BF16),) * chips,
        in_specs=[IN_HBM],
        out_specs=(IN_VMEM,) * chips,
        scratch_shapes=[
            pltpu.VMEM(frames.shape, BF16),
            pltpu.VMEM((rows + 2, count * cols, chans), F32),
            pltpu.SemaphoreType.DMA(()),
        ],
        name="pack",
        compiler_params=limit(8),
        cost_estimate=pl.CostEstimate(flops=20_000_000_000, transcendentals=0, bytes_accessed=2 * frames.size),
    )(*in_hbm(frames))


def project_kernel(cot_hbm, up_hbm, mate, g, hidden_grad, cot, up, wide, sems):
    copies = [
        pltpu.make_async_copy(cot_hbm, cot, sems.at[0]),
        pltpu.make_async_copy(up_hbm, up, sems.at[1]),
    ]
    for copy in copies:
        copy.start()
    slots, frames, own, cols, _ = cot.shape
    mine = here() % 2
    for source, core in ((mate, 1 - mine), (cot, mine)):
        if source is cot:
            copies[0].wait()
        for s in range(slots):
            for t in range(frames):
                for q in range(own):
                    base = (s * frames + t) * cols
                    wide[core, q, base : base + cols, :] = source[s, t, q].astype(F32)
    value = wide[...].reshape(g.shape).astype(BF16)
    g[...] = value
    copies[1].wait()
    hidden_grad[...] = lax.dot_general(value, up[...], NT, preferred_element_type=F32).astype(BF16)


def project(cot, up, mate):
    slots, count, own, cols, width = cot.shape
    places = 2 * slots * count * own * cols
    return pl.pallas_call(
        project_kernel,
        out_shape=(struct((places, width), BF16), struct((places, up.shape[0]), BF16)),
        in_specs=[IN_HBM, IN_HBM, IN_VMEM],
        out_specs=(IN_VMEM,) * 2,
        scratch_shapes=[
            pltpu.VMEM(cot.shape, BF16),
            pltpu.VMEM(up.shape, BF16),
            pltpu.VMEM((2, own, slots * count * cols, width), F32),
            pltpu.SemaphoreType.DMA((2,)),
        ],
        name="project",
        compiler_params=limit(16),
    )(*in_hbm(cot, up), mate)


def gather_kernel(*refs):
    parts, out = refs[:-1], refs[-1]
    me = here() // 2
    for k, part in enumerate(parts):
        out[me ^ k] = part[...]


def gather(parts):
    return pl.pallas_call(
        gather_kernel,
        out_shape=struct((len(parts),) + parts[0].shape, BF16),
        in_specs=[IN_VMEM] * len(parts),
        out_specs=IN_VMEM,
        name="gather",
        compiler_params=limit(4),
    )(*parts)


def by_parity(chans, size):
    row = lax.broadcasted_iota(jnp.int32, (chans, chans), 0)
    col = lax.broadcasted_iota(jnp.int32, (chans, chans), 1)
    block = row // size
    target = (block % 2) * (chans // 2) + (block // 2) * size + row % size
    return jnp.where(target == col, 1.0, 0.0).astype(BF16)


def rows_kernel(size, cols, direct, half_ref, other, weight, g, hidden_grad, *refs):
    chips, tall, block, chans = half_ref.shape
    near = tall - 2
    *outs, field, hidden, grads, term = refs
    backs, outs = outs[:chips], outs[chips:]
    length = 2 * chips * block
    base = up_to(2 * cols + 1, 8)
    me = here() // 2
    mine = here() % 2
    for source, core in ((half_ref, mine), (other, 1 - mine)):
        for z in range(chips):
            start = pl.multiple_of(base + (2 * z + core) * block, 8)
            for i in range(tall):
                field[i, pl.ds(start, block), :] = source[z, i].astype(F32)
    for t in range(1, 3):
        field[:, base - t * cols : base - (t - 1) * cols, :] = field[:, base : base + cols, :]
    total = jnp.zeros((near * length, chans), F32)
    for a in range(3):
        flats = []
        for c in range(3):
            start = base + (a - 2) * cols + c - 1
            flats.append(column_shift(field[:, start : start + length, :], cols, c - 1))
        left = jnp.concatenate(
            [
                flats[c][b : b + near].reshape(near * length, chans)
                for b in range(3)
                for c in range(3)
            ],
            axis=1,
        )
        right = weight[9 * a : 9 * a + 9].reshape(9 * chans, chans)
        total += jnp.dot(left, right, preferred_element_type=F32)
    sigma = 1.0 / (1.0 + jnp.exp(-total))
    ordered = jnp.dot(
        (total * sigma).astype(BF16), by_parity(chans, size), preferred_element_type=F32
    ).astype(BF16)
    half = chans // 2
    for p in range(2):
        hidden[p] = ordered[:, p * half : (p + 1) * half]
    product = lax.dot_general(hidden[mine], g[...], TN, preferred_element_type=F32)
    parts, _, lanes = term.shape
    for n in range(parts):
        term[n] = product[:, n * lanes : (n + 1) * lanes]
    if direct:
        spot = lax.axis_index(("dp", "rep"))
        outs[0][...] = term[spot]
        for k in range(1, parts):
            outs[k][...] = term[spot ^ k].astype(BF16)
    else:
        outs[0][...] = term[...]
    slope = sigma * (1.0 + total * (1.0 - sigma))
    value = (hidden_grad[...].astype(F32) * slope).astype(BF16).astype(F32)
    grads[:, :length, :] = value.reshape(near, length, chans)
    grads[:, length:, :] = jnp.zeros((near, grads.shape[1] - length, chans), F32)
    for k, back in enumerate(backs):
        start = pl.multiple_of((2 * (me ^ k) + mine) * block, 8)
        back[...] = grads[:, pl.ds(start, back.shape[1]), :].astype(BF16)


def rows_of(half_ref, other, weight, g, hidden_grad, size, cols, parts, direct):
    chips, tall, block, chans = half_ref.shape
    near = tall - 2
    length = 2 * chips * block
    lanes = g.shape[1] // parts
    half = chans // 2
    reach = block + 2 * cols
    if direct:
        outs = (struct((half, lanes), F32),) + (struct((half, lanes), BF16),) * (parts - 1)
    else:
        outs = (struct((parts, half, lanes), F32),)
    outs = (struct((near, reach, chans), BF16),) * chips + outs
    return pl.pallas_call(
        functools.partial(rows_kernel, size, cols, direct),
        out_shape=outs,
        in_specs=[IN_VMEM] * 5,
        out_specs=(IN_VMEM,) * len(outs),
        scratch_shapes=[
            pltpu.VMEM((tall, up_to(up_to(2 * cols + 1, 8) + length + 1, 8), chans), F32),
            pltpu.VMEM((2, near * length, half), BF16),
            pltpu.VMEM((near, up_to(length + 2 * cols, 8), chans), F32),
            pltpu.VMEM((parts, half, lanes), F32),
        ],
        name="rows",
        compiler_params=limit(32),
    )(half_ref, other, weight, g, hidden_grad)


def spread_kernel(size, received, mine, *refs):
    got, kept, sends = refs[:received], refs[received], refs[received + 1 :]

    def total(block):
        rows = pl.ds(pl.multiple_of(block * size, size), size)
        value = mine[rows, :]
        for ref in got:
            value = value + ref[rows, :].astype(F32)
        return value

    me = here() // 2
    kept[...] = total(me)
    for k, send in enumerate(sends, 1):
        send[...] = total(me ^ k).astype(BF16)


def spread(mine, got, size):
    half, width = mine.shape
    chips = half // size
    return pl.pallas_call(
        functools.partial(spread_kernel, size, len(got)),
        out_shape=(struct((size, width), F32),) + (struct((size, width), BF16),) * (chips - 1),
        in_specs=[IN_VMEM] * (1 + len(got)),
        out_specs=(IN_VMEM,) * chips,
        name="split_rows",
        compiler_params=limit(4),
    )(mine, *got)


def final_kernel(factor, mine, *refs):
    value = mine[...]
    for ref in refs[:-1]:
        value = value + ref[...].astype(F32)
    refs[-1][...] = value * factor


def final(mine, got, factor):
    return pl.pallas_call(
        functools.partial(final_kernel, factor),
        out_shape=struct(mine.shape, F32),
        in_specs=[IN_VMEM] * (1 + len(got)),
        out_specs=IN_VMEM,
        name="final_sum",
        compiler_params=limit(4),
    )(mine, *got)


def finish_kernel(weight, own, *refs):
    got, (out, field) = refs[:-2], refs[-2:]
    frames, rows, cols, chans = out.shape
    near, reach, _ = own.shape
    me = here() // 2
    for i in range(near):
        field[me * near + i, 8 : 8 + reach, :] = own[i].astype(F32)
        for k, ref in enumerate(got, 1):
            field[(me ^ k) * near + i, 8 : 8 + reach, :] = ref[i].astype(F32)
    span = up_to(reach, 16)
    sums = [jnp.zeros((rows * span, chans), F32)] * 3
    for c in range(3):
        block = column_shift(field[:, 9 - c : 9 - c + span, :], cols, 1 - c)
        flat = block.reshape(rows * span, chans)
        for b in range(3):
            left = row_shift(flat, span, 1 - b)
            for a in range(3):
                sums[a] += lax.dot_general(
                    left, weight[9 * a + 3 * b + c], NT, preferred_element_type=F32
                )
    sums = [value.reshape(rows, span, chans) for value in sums]

    def at(a, t):
        return sums[a][:, t * cols : (t + 1) * cols]

    edge = jnp.where(here() == 0, at(0, 0) + at(0, 1) + at(1, 0), 0.0)
    for t in range(frames):
        value = at(0, t + 2) + at(1, t + 1) + at(2, t)
        if t == 0:
            value = value + edge
        out[t] = value.astype(BF16)


def finish(weight, own, got, shape):
    _, rows, _, chans = shape
    return pl.pallas_call(
        finish_kernel,
        out_shape=struct(shape, BF16),
        in_specs=[IN_VMEM] * (2 + len(got)),
        out_specs=IN_VMEM,
        scratch_shapes=[pltpu.VMEM((rows, 16 + up_to(own.shape[1], 16), chans), F32)],
        name="finish",
        compiler_params=limit(16),
    )(weight, own, *got)


def whole(clip_frames, conv_weight, up_weight, cotangent):
    frames_local = clip_frames[0]
    frames, rows, cols, chans = frames_local.shape
    width = up_weight.shape[1]
    time_count = lax.axis_size("tm")
    clip_count = lax.axis_size(("dp", "rep"))
    weight = conv_weight.reshape(27, chans, chans)
    factor = 1.0 / math.sqrt(clip_count * frames * time_count * rows * cols)
    size = chans // time_count
    chips = time_count // 2
    own_rows = rows // time_count
    direct = clip_count <= DIRECT and chips <= DIRECT and width == clip_count * chans

    cot = cotangent.reshape(time_count, frames, own_rows, cols, width)
    mate = swap(cot, "tm", 1)
    parts = pack(frames_local, 2 * own_rows, chips)
    arrived = swaps(parts[1:], "tm", 2)
    half = gather([parts[0]] + arrived)
    other = swap(half, "tm", 1)
    g, hidden_grad = project(cot, up_weight, mate)
    outs = rows_of(half, other, weight, g, hidden_grad, size, cols, clip_count, direct)
    (own, *backs), (mine, *sends) = outs[:chips], outs[chips:]
    returned = swaps(backs, "tm", 2)
    if direct:
        arrived = swaps(sends, ("dp", "rep"), 1)
        kept, *sends = spread(mine, arrived, size)
        arrived = swaps(sends, "tm", 2)
        summed = final(kept, arrived, factor)
    else:
        value = lax.psum_scatter(mine, ("dp", "rep"), scatter_dimension=0, tiled=True)[0]
        pairs = [[s for s in range(time_count) if s % 2 == c] for c in range(2)]
        value = lax.psum_scatter(
            value, "tm", scatter_dimension=0, axis_index_groups=pairs, tiled=True
        )
        summed = value * factor
    input_grad = finish(weight, own, returned, frames_local.shape)
    return (input_grad[None], summed)


def solution(mesh):
    in_specs = (
        P(("dp", "rep"), "tm", None, None, None),
        P(),
        P(),
        P(("dp", "rep"), None, "tm", None, None),
    )
    out_specs = (P(("dp", "rep"), "tm", None, None, None), P("tm", ("dp", "rep")))
    return jax.shard_map(whole, mesh=mesh, in_specs=in_specs, out_specs=out_specs, check_vma=False)
```
